32 devices in a mesh: row: 8 (over y, x, core), col: 4 (over z).
Axes of the slice: x: 2, y: 2, z: 4, core: 2. Of those that a mesh axis runs over, the one named last changes fastest.
Arguments:
- left_factors: float32 [128, 256, 32], P(None, ('row', 'col')), may hold values from -12 to 12
- right_factors: float32 [128, 128, 32], P(None, ('col', 'row')), may hold values from -12 to 12
- weight: float32 [1024, 128], replicated, may hold values from -0.1875 to 0.1875
- bias: float32 [128], replicated, may hold values from -2 to 2
- cotangent: float32 [256, 128, 128], P('row', 'col'), may hold values from -6 to 6
Outputs:
- pair_out: float32 [256, 128, 128], P('row', 'col')
- left_grad: float32 [128, 256, 32], P(None, ('row', 'col'))
- right_grad: float32 [128, 128, 32], P(None, ('col', 'row'))
- weight_grad: float32 [1024, 128], replicated
- bias_grad: float32 [128], replicated
The draws below stay inside these ranges and needn't reach their ends.
All inputs are finite; a program needn't handle non-finite values.
Results may differ from the reference program's by a relative error of at most 0.0001.
Values sent between devices are 32-bit elements; how exact they have to be, the bound alone decides.
A program may use at most 64 MiB of HBM per device.

```python
import jax
import jax.numpy as jnp
from jax import lax

S = 128
C = 32
CZ = 128
NI = 256
NJ = 128


def block_scale(rng, extent, cuts, low, high):
    def one(dim, blocks):
        steps = jax.random.uniform(jax.random.fold_in(jax.random.fold_in(rng, 6), dim), (blocks,), jnp.float32, low / len(cuts), high / len(cuts))
        return jnp.repeat(jnp.exp(steps), extent[dim] // blocks).reshape((-1,) + (1,) * (len(extent) - dim - 1))

    level = one(*cuts[0])
    for cut in cuts[1:]:
        level = level * one(*cut)
    return level


def noise(rng, shape, deviation, limit, shards=(), dtype=jnp.bfloat16):
    loudness = block_scale(rng, shape, shards, -0.22, 0.18) if shards else 1.0
    drawn = jax.random.normal(rng, shape, jnp.float32) * deviation * loudness
    return jnp.minimum(jnp.maximum(drawn, -limit), limit).astype(dtype)


def setup_inputs(seed: int = 0) -> dict:
    arg_keys = jax.random.split(jax.random.key(seed), 6)
    return {
        "left_factors": noise(arg_keys[0], (S, NI, C), 2.0, 12.0, ((1, 32),), jnp.float32),
        "right_factors": noise(arg_keys[1], (S, NJ, C), 2.0, 12.0, ((1, 32),), jnp.float32),
        "weight": noise(arg_keys[2], (C * C, CZ), (C * C) ** -0.5, 0.1875, (), jnp.float32),
        "bias": noise(arg_keys[3], (CZ,), 0.3, 2.0, (), jnp.float32),
        "cotangent": noise(arg_keys[4], (NI, NJ, CZ), 1.0, 6.0, ((0, 8), (1, 4)), jnp.float32),
    }


def reference(left_factors, right_factors, weight, bias, cotangent):
    high = lax.Precision.HIGHEST
    step_rows = 16
    blocks = NI // step_rows
    left_blocks = left_factors.reshape(S, blocks, step_rows, C).transpose(1, 0, 2, 3)
    cot_blocks = cotangent.reshape(blocks, step_rows, NJ, CZ)

    def visit(carry, item):
        weight_sum, right_sum = carry
        left_block, cot_block = item
        outer = jnp.einsum("sic,sjd->ijcd", left_block, right_factors, precision=high) / S
        flat = outer.reshape(step_rows, NJ, C * C)
        pair_block = jnp.einsum("ijk,ke->ije", flat, weight, precision=high) + bias
        grad_flat = jnp.einsum("ije,ke->ijk", cot_block, weight, precision=high)
        weight_sum = weight_sum + jnp.einsum("ijk,ije->ke", flat, cot_block, precision=high)
        grad_outer = grad_flat.reshape(step_rows, NJ, C, C)
        left_block_grad = jnp.einsum("ijcd,sjd->sic", grad_outer, right_factors, precision=high) / S
        right_sum = right_sum + jnp.einsum("ijcd,sic->sjd", grad_outer, left_block, precision=high) / S
        return (weight_sum, right_sum), (pair_block, left_block_grad)

    start = (jnp.zeros((C * C, CZ), jnp.float32), jnp.zeros((S, NJ, C), jnp.float32))
    (weight_sum, right_grad), (pair_blocks, left_parts) = lax.scan(visit, start, (left_blocks, cot_blocks))
    pair_out = pair_blocks.reshape(NI, NJ, CZ)
    left_grad = left_parts.transpose(1, 0, 2, 3).reshape(S, NI, C)
    weight_grad = weight_sum / NI
    bias_grad = jnp.sum(cotangent, axis=(0, 1)) / NI
    return pair_out, left_grad, right_grad, weight_grad, bias_grad
```

```python
import functools

import jax
import jax.numpy as jnp
from jax import lax
from jax.experimental import pallas as pl
from jax.experimental.pallas import tpu as pltpu
from jax.sharding import PartitionSpec as P

F32 = jnp.float32
BF16 = jnp.bfloat16
MESH = pl.DeviceIdType.MESH
VMEM = pl.BlockSpec(memory_space=pltpu.VMEM)
ROWS_PER_STEP = 8


def split(x):
    high = x.astype(BF16)
    return high, (x - high.astype(F32)).astype(BF16)


def dot(a, b):
    return lax.dot_general(a, b, (((1,), (0,)), ((), ())), preferred_element_type=F32)


def dot3(a_high, a_low, b_high, b_low):
    return dot(a_high, b_high) + (dot(a_high, b_low) + dot(a_low, b_high))


def swap_groups(pieces):
    lane = lax.broadcasted_iota(jnp.int32, pieces[0].shape, 1)
    low = lane < 64
    even = (lane & 32) == 0

    def far(a, b):
        moved = pltpu.roll(jnp.where(low, b, a), 64, 1)
        return jnp.where(low, a, moved), jnp.where(low, moved, b)

    def near(a, b):
        return (
            jnp.where(even, a, pltpu.roll(b, 32, 1)),
            jnp.where(even, pltpu.roll(a, 96, 1), b),
        )

    p0, p2 = far(pieces[0], pieces[2])
    p1, p3 = far(pieces[1], pieces[3])
    p0, p1 = near(p0, p1)
    p2, p3 = near(p2, p3)
    return p0, p1, p2, p3


def gather_kernel(nrow, ncol, l_ref, r_ref, lo_ref, ro_ref, ls, lr, rs, rr):
    row, col = lax.axis_index("row"), lax.axis_index("col")
    barrier = pltpu.get_barrier_semaphore()

    @pl.loop(1, ncol)
    def _(k):
        pl.semaphore_signal(
            barrier, inc=1, device_id={"row": row, "col": lax.rem(col + k, ncol)}, device_id_type=MESH
        )

    @pl.loop(1, nrow)
    def _(k):
        pl.semaphore_signal(
            barrier, inc=1, device_id={"row": lax.rem(row + k, nrow), "col": col}, device_id_type=MESH
        )

    pl.semaphore_wait(barrier, nrow + ncol - 2)

    def left_copy(k):
        return pltpu.make_async_remote_copy(
            src_ref=l_ref, dst_ref=lo_ref.at[col], send_sem=ls.at[k], recv_sem=lr.at[k],
            device_id={"row": row, "col": lax.rem(col + k, ncol)}, device_id_type=MESH,
        )

    def right_copy(k):
        return pltpu.make_async_remote_copy(
            src_ref=r_ref, dst_ref=ro_ref.at[row], send_sem=rs.at[k], recv_sem=rr.at[k],
            device_id={"row": lax.rem(row + k, nrow), "col": col}, device_id_type=MESH,
        )

    @pl.loop(1, ncol)
    def _(k):
        left_copy(k).start()

    @pl.loop(1, nrow)
    def _(k):
        right_copy(k).start()

    lo_ref[col] = l_ref[...]
    ro_ref[row] = r_ref[...]

    @pl.loop(1, ncol)
    def _(k):
        left_copy(k).wait()

    @pl.loop(1, nrow)
    def _(k):
        right_copy(k).wait()


def compute_kernel(
    width, lo_ref, ro_ref, w_ref, b_ref, cot_ref,
    pair_ref, lp_ref, rp_ref, wp_ref,
    l_h, l_l, lt_h, lt_l, r_h, r_l, rt_h, rt_l, w_h, w_l, wt_h, wt_l,
    rows_scr, out_scr, t_h, t_l, h_h, h_l, wsum, rsum, lsum,
):
    ncol, samples, lw = lo_ref.shape
    nrow, _, rw = ro_ref.shape
    tile_rows, tile_cols = ncol * lw // width, nrow * rw // width
    channels = width * width
    scale = 1.0 / samples
    per = 128 // width

    for k in range(ncol):
        lsum[:, k * lw : (k + 1) * lw] = lo_ref[k]
    left = lsum[...]
    l_h[...], l_l[...] = split(left)
    lt_h[...], lt_l[...] = split(left.T)
    for k in range(nrow):
        rows_scr[k * rw : (k + 1) * rw, :] = ro_ref[k].T
    for d in range(width):
        rsum[d * tile_cols : (d + 1) * tile_cols, :] = rows_scr[pl.ds(d, tile_cols, stride=width), :]
    right = rsum[...]
    rt_h[...], rt_l[...] = split(right)
    r_h[...], r_l[...] = split(right.T)
    for d in range(width):
        rows_scr[d * width : (d + 1) * width, :] = w_ref[pl.ds(d, width, stride=width), :]
    weight = rows_scr[0:channels, :]
    w_h[...], w_l[...] = split(weight)
    wt_h[...], wt_l[...] = split(weight.T)

    wsum[...] = jnp.zeros_like(wsum)
    rsum[...] = jnp.zeros_like(rsum)
    step_lanes = ROWS_PER_STEP * width
    step_rows = ROWS_PER_STEP * tile_cols
    halves = step_lanes // 128

    def step(g, bias_sum):
        lanes = pl.ds(pl.multiple_of(g * step_lanes, step_lanes), step_lanes)
        rows = pl.ds(pl.multiple_of(g * step_rows, step_rows), step_rows)
        cot = cot_ref[rows, :]
        cot_h, cot_l = split(cot)
        cott_h, cott_l = split(cot.T)
        out_scr[...] = dot3(rt_h[...], rt_l[...], l_h[:, lanes], l_l[:, lanes]) * scale
        for block in range(width // per):
            for half in range(halves):
                pieces = [
                    out_scr[(block * per + a) * tile_cols : (block * per + a + 1) * tile_cols,
                            half * 128 : (half + 1) * 128]
                    for a in range(per)
                ]
                for a, piece in enumerate(swap_groups(pieces)):
                    at = (half * per + a) * tile_cols
                    high, low = split(piece)
                    t_h[at : at + tile_cols, block * 128 : (block + 1) * 128] = high
                    t_l[at : at + tile_cols, block * 128 : (block + 1) * 128] = low
        pair_ref[rows, :] = dot3(t_h[...], t_l[...], w_h[...], w_l[...]) + b_ref[...]
        wsum[...] += dot3(cott_h, cott_l, t_h[...], t_l[...])
        grad = dot3(cot_h, cot_l, wt_h[...], wt_l[...]) * scale
        for block in range(width // per):
            for half in range(halves):
                pieces = [
                    grad[(half * per + a) * tile_cols : (half * per + a + 1) * tile_cols,
                         block * 128 : (block + 1) * 128]
                    for a in range(per)
                ]
                for a, piece in enumerate(swap_groups(pieces)):
                    at = (block * per + a) * tile_cols
                    high, low = split(piece)
                    h_h[at : at + tile_cols, half * 128 : (half + 1) * 128] = high
                    h_l[at : at + tile_cols, half * 128 : (half + 1) * 128] = low
        lsum[:, lanes] = dot3(r_h[...], r_l[...], h_h[...], h_l[...])
        rsum[...] += dot3(h_h[...], h_l[...], lt_h[lanes, :], lt_l[lanes, :])
        return bias_sum + jnp.sum(cot, axis=0, keepdims=True)

    bias_sum = lax.fori_loop(
        0, tile_rows // ROWS_PER_STEP, step, jnp.zeros((1, cot_ref.shape[1]), F32)
    )

    for k in range(ncol):
        lp_ref[k] = lsum[:, k * lw : (k + 1) * lw]
    for d in range(width):
        rows_scr[pl.ds(d, tile_cols, stride=width), :] = rsum[d * tile_cols : (d + 1) * tile_cols, :]
    for k in range(nrow):
        rp_ref[k] = rows_scr[k * rw : (k + 1) * rw, :].T
    turned = wsum[...].T
    for d in range(width):
        rows_scr[pl.ds(d, width, stride=width), :] = turned[d * width : (d + 1) * width, :]
    devices, chunk, cols = wp_ref.shape
    share = channels // devices
    tail = jnp.broadcast_to(bias_sum, (8, cols))
    for q in range(devices):
        wp_ref[q, 0:share, :] = rows_scr[q * share : (q + 1) * share, :]
        wp_ref[q, share:chunk, :] = tail


def reduce_kernel(
    nrow, ncol, total_rows, lp_ref, rp_ref, wp_ref, lg_ref, rg_ref, wg_ref, bg_ref,
    lbuf, rbuf, wbuf, ls, lr, rs, rr, ws, wr, gs, gr,
):
    row, col = lax.axis_index("row"), lax.axis_index("col")
    n = nrow * ncol
    me = row * ncol + col
    share = wg_ref.shape[1]

    def device(k):
        p = lax.rem(me + k, n)
        return {"row": p // ncol, "col": lax.rem(p, ncol)}

    barrier = pltpu.get_barrier_semaphore()

    @pl.loop(1, n)
    def _(k):
        pl.semaphore_signal(barrier, inc=1, device_id=device(k), device_id_type=MESH)

    pl.semaphore_wait(barrier, n - 1)

    def weight_copy(k):
        return pltpu.make_async_remote_copy(
            src_ref=wp_ref.at[lax.rem(me + k, n)], dst_ref=wbuf.at[me],
            send_sem=ws.at[k], recv_sem=wr.at[k], device_id=device(k), device_id_type=MESH,
        )

    def whole_copy(k):
        return pltpu.make_async_remote_copy(
            src_ref=wg_ref.at[me], dst_ref=wg_ref.at[me],
            send_sem=gs.at[k], recv_sem=gr.at[k], device_id=device(k), device_id_type=MESH,
        )

    def left_copy(k):
        peer = lax.rem(col + k, ncol)
        return pltpu.make_async_remote_copy(
            src_ref=lp_ref.at[peer], dst_ref=lbuf.at[col], send_sem=ls.at[k], recv_sem=lr.at[k],
            device_id={"row": row, "col": peer}, device_id_type=MESH,
        )

    def right_copy(k):
        peer = lax.rem(row + k, nrow)
        return pltpu.make_async_remote_copy(
            src_ref=rp_ref.at[peer], dst_ref=rbuf.at[row], send_sem=rs.at[k], recv_sem=rr.at[k],
            device_id={"row": peer, "col": col}, device_id_type=MESH,
        )

    def each(count, act):
        pl.loop(1, count)(act)

    each(n, lambda k: weight_copy(k).start())
    each(ncol, lambda k: left_copy(k).start())
    each(nrow, lambda k: right_copy(k).start())
    wbuf[me] = wp_ref[me]
    lbuf[col] = lp_ref[col]
    rbuf[row] = rp_ref[row]
    each(n, lambda k: weight_copy(k).wait())
    total = lax.fori_loop(1, n, lambda q, acc: acc + wbuf[q], wbuf[0]) / total_rows
    wg_ref[me] = total[0:share, :]
    bg_ref[...] = total[share : share + 1, :]
    each(n, lambda k: whole_copy(k).start())
    each(ncol, lambda k: left_copy(k).wait())
    lg_ref[...] = functools.reduce(lambda a, b: a + b, [lbuf[q] for q in range(ncol)])
    each(nrow, lambda k: right_copy(k).wait())
    rg_ref[...] = functools.reduce(lambda a, b: a + b, [rbuf[q] for q in range(nrow)])
    each(n, lambda k: whole_copy(k).wait())


def per_device(nrow, ncol, left_factors, right_factors, weight, bias, cotangent):
    samples, li, width = left_factors.shape
    rj = right_factors.shape[1]
    tile_rows, tile_cols, pair_width = cotangent.shape
    channels = weight.shape[0]
    n = nrow * ncol
    lw, rw = li * width, rj * width
    share = channels // n
    dma = pltpu.SemaphoreType.DMA

    def shape(*dims):
        return jax.ShapeDtypeStruct(dims, F32)

    lo, ro = pl.pallas_call(
        functools.partial(gather_kernel, nrow, ncol),
        out_shape=(shape(ncol, samples, lw), shape(nrow, samples, rw)),
        in_specs=[VMEM] * 2,
        out_specs=[VMEM] * 2,
        scratch_shapes=[dma((ncol,)), dma((ncol,)), dma((nrow,)), dma((nrow,))],
        compiler_params=pltpu.CompilerParams(collective_id=0, has_side_effects=True),
        name="gather",
    )(left_factors.reshape(samples, lw), right_factors.reshape(samples, rw))

    lanes, rows = tile_rows * width, tile_cols * width
    big = max(rows, channels)
    step_lanes, step_rows = ROWS_PER_STEP * width, ROWS_PER_STEP * tile_cols
    scratch = [
        pltpu.VMEM(dims, dtype)
        for dims, dtype in [
            ((samples, lanes), BF16), ((samples, lanes), BF16),
            ((lanes, samples), BF16), ((lanes, samples), BF16),
            ((samples, rows), BF16), ((samples, rows), BF16),
            ((rows, samples), BF16), ((rows, samples), BF16),
            ((channels, pair_width), BF16), ((channels, pair_width), BF16),
            ((pair_width, channels), BF16), ((pair_width, channels), BF16),
            ((big, 128), F32), ((rows, step_lanes), F32),
            ((step_rows, channels), BF16), ((step_rows, channels), BF16),
            ((rows, step_lanes), BF16), ((rows, step_lanes), BF16),
            ((pair_width, channels), F32), ((rows, samples), F32), ((samples, lanes), F32),
        ]
    ]
    pair, lp, rp, wp = pl.pallas_call(
        functools.partial(compute_kernel, width),
        out_shape=(
            shape(tile_rows * tile_cols, pair_width),
            shape(ncol, samples, lw),
            shape(nrow, samples, rw),
            shape(n, share + 8, pair_width),
        ),
        in_specs=[VMEM] * 5,
        out_specs=[VMEM] * 4,
        scratch_shapes=scratch,
        name="tile",
    )(lo, ro, weight, bias.reshape(1, pair_width), cotangent.reshape(tile_rows * tile_cols, pair_width))

    lg, rg, wg, bg = pl.pallas_call(
        functools.partial(reduce_kernel, nrow, ncol, tile_rows * nrow),
        out_shape=(
            shape(samples, lw), shape(samples, rw), shape(n, share, pair_width), shape(1, pair_width),
        ),
        in_specs=[VMEM] * 3,
        out_specs=[VMEM] * 4,
        scratch_shapes=[
            pltpu.VMEM((ncol, samples, lw), F32),
            pltpu.VMEM((nrow, samples, rw), F32),
            pltpu.VMEM((n, share + 8, pair_width), F32),
            dma((ncol,)), dma((ncol,)), dma((nrow,)), dma((nrow,)),
            dma((n,)), dma((n,)), dma((n,)), dma((n,)),
        ],
        compiler_params=pltpu.CompilerParams(collective_id=1, has_side_effects=True),
        name="reduce",
    )(lp, rp, wp)
    return (
        pair.reshape(tile_rows, tile_cols, pair_width),
        lg.reshape(samples, li, width),
        rg.reshape(samples, rj, width),
        wg.reshape(channels, pair_width),
        bg.reshape(pair_width),
    )


def solution(mesh):
    nrow, ncol = mesh.shape["row"], mesh.shape["col"]
    in_specs = (
        P(None, ("row", "col"), None),
        P(None, ("col", "row"), None),
        P(),
        P(),
        P("row", "col", None),
    )
    out_specs = (
        P("row", "col", None),
        P(None, ("row", "col"), None),
        P(None, ("col", "row"), None),
        P(),
        P(),
    )
    return jax.shard_map(
        functools.partial(per_device, nrow, ncol),
        mesh=mesh, in_specs=in_specs, out_specs=out_specs, check_vma=False,
    )
```

```python
import functools

import jax
import jax.numpy as jnp
from jax import lax
from jax.experimental import pallas as pl
from jax.experimental.pallas import tpu as pltpu
from jax.sharding import PartitionSpec as P

F32 = jnp.float32
BF16 = jnp.bfloat16
MESH = pl.DeviceIdType.MESH
VMEM = pl.BlockSpec(memory_space=pltpu.VMEM)
STEP = 8


def split(x):
    high = x.astype(BF16)
    return high, (x - high.astype(F32)).astype(BF16)


def dot(a, b):
    return lax.dot_general(a, b, (((1,), (0,)), ((), ())), preferred_element_type=F32)


def dot3(a_high, a_low, b_high, b_low):
    return dot(a_high, b_high) + (dot(a_high, b_low) + dot(a_low, b_high))


def swap_groups(pieces):
    lane = lax.broadcasted_iota(jnp.int32, pieces[0].shape, 1)
    low = lane < 64
    even = (lane & 32) == 0

    def far(a, b):
        moved = pltpu.roll(jnp.where(low, b, a), 64, 1)
        return jnp.where(low, a, moved), jnp.where(low, moved, b)

    def near(a, b):
        return (
            jnp.where(even, a, pltpu.roll(b, 32, 1)),
            jnp.where(even, pltpu.roll(a, 96, 1), b),
        )

    p0, p2 = far(pieces[0], pieces[2])
    p1, p3 = far(pieces[1], pieces[3])
    p0, p1 = near(p0, p1)
    p2, p3 = near(p2, p3)
    return p0, p1, p2, p3


def tile_kernel(
    nrow, ncol, width, l_ref, r_ref, w_ref, b_ref, cot_ref,
    pair_ref, lg_ref, rg_ref, wg_ref, bg_ref,
    lo, ro, lp, lbuf, rp, rbuf, wp, wbuf, part,
    l_h, l_l, lt_h, lt_l, r_h, r_l, rt_h, rt_l, w_h, w_l, wt_h, wt_l,
    c_h, c_l, ct_h, ct_l, h_h, h_l, o_scr, t_h, t_l, tmp,
    gls, glr, grs, grr, ls, lr, rs, rr, ws, wr, vs, vr, us, ur, xs, xr,
):
    row, col = lax.axis_index("row"), lax.axis_index("col")
    lw, samples = l_ref.shape
    rw = r_ref.shape[0]
    tile_rows, tile_cols = ncol * lw // width, nrow * rw // width
    channels, pair_width = w_ref.shape
    scale = 1.0 / samples
    per = 128 // width
    chunk = channels // nrow
    share = channels // (nrow * ncol)

    def in_row(peer):
        return {"row": peer, "col": col}

    def in_col(peer):
        return {"row": row, "col": peer}

    def block(ref, index, size):
        return ref.at[pl.ds(pl.multiple_of(index * size, size), size)]

    def each(count, here, act):
        @pl.loop(1, count)
        def _(k):
            act(lax.rem(here + k, count))

    def send(src, dst, send_sem, recv_sem, device):
        return pltpu.make_async_remote_copy(
            src_ref=src, dst_ref=dst, send_sem=send_sem, recv_sem=recv_sem,
            device_id=device, device_id_type=MESH,
        )

    def left_gather(peer, slot):
        return send(l_ref, block(lo, slot, lw), gls.at[peer], glr.at[slot], in_col(peer))

    def right_gather(peer, slot):
        return send(r_ref, block(ro, slot, rw), grs.at[peer], grr.at[slot], in_row(peer))

    def left_term(peer, slot):
        return send(block(lp, peer, lw), lbuf.at[slot], ls.at[peer], lr.at[slot], in_col(peer))

    def right_term(peer, slot):
        return send(block(rp, peer, rw), rbuf.at[slot], rs.at[peer], rr.at[slot], in_row(peer))

    def weight_row_term(peer, slot):
        return send(wp.at[peer], wbuf.at[slot], ws.at[peer], wr.at[slot], in_row(peer))

    def weight_col_term(peer, slot):
        return send(part.at[0, peer], part.at[1, slot], vs.at[peer], vr.at[slot], in_col(peer))

    def weight_col_whole(peer, slot):
        return send(wg_ref.at[row, col], wg_ref.at[row, slot], us.at[peer], ur.at[slot], in_col(peer))

    def weight_row_whole(peer, slot):
        return send(wg_ref.at[row], wg_ref.at[slot], xs.at[peer], xr.at[slot], in_row(peer))

    barrier = pltpu.get_barrier_semaphore()
    each(ncol, col, lambda p: pl.semaphore_signal(
        barrier, inc=1, device_id=in_col(p), device_id_type=MESH))
    each(nrow, row, lambda p: pl.semaphore_signal(
        barrier, inc=1, device_id=in_row(p), device_id_type=MESH))
    pl.semaphore_wait(barrier, nrow + ncol - 2)
    each(ncol, col, lambda p: left_gather(p, col).start())
    each(nrow, row, lambda p: right_gather(p, row).start())

    for d in range(width):
        tmp[d * width : (d + 1) * width, :] = w_ref[pl.ds(d, width, stride=width), :]
    weight = tmp[0:channels, :]
    w_h[...], w_l[...] = split(weight)
    wt_h[...], wt_l[...] = split(weight.T)
    cot = cot_ref[...]
    c_h[...], c_l[...] = split(cot)
    ct_h[...], ct_l[...] = split(cot.T)
    bias_tail = jnp.broadcast_to(jnp.sum(cot, axis=0, keepdims=True), (8, pair_width))
    pair_ref[...] = jnp.broadcast_to(b_ref[...], pair_ref.shape)

    step_lanes, step_rows = STEP * width, STEP * tile_cols
    halves = step_lanes // 128

    @pl.loop(0, tile_rows // STEP)
    def _(g):
        rows = pl.ds(pl.multiple_of(g * step_rows, step_rows), step_rows)
        grad = dot3(c_h[rows, :], c_l[rows, :], wt_h[...], wt_l[...]) * scale
        for b in range(width // per):
            for half in range(halves):
                pieces = [
                    grad[(half * per + a) * tile_cols : (half * per + a + 1) * tile_cols,
                         b * 128 : (b + 1) * 128]
                    for a in range(per)
                ]
                lanes = pl.ds(pl.multiple_of(g * step_lanes + half * 128, 128), 128)
                for a, piece in enumerate(swap_groups(pieces)):
                    at = (b * per + a) * tile_cols
                    high, low = split(piece)
                    h_h[at : at + tile_cols, lanes] = high
                    h_l[at : at + tile_cols, lanes] = low

    ro[pl.ds(pl.multiple_of(row * rw, rw), rw), :] = r_ref[...]
    each(nrow, row, lambda p: right_gather(p, p).wait())
    for d in range(width):
        tmp[d * tile_cols : (d + 1) * tile_cols, :] = ro[pl.ds(d, tile_cols, stride=width), :]
    right = tmp[0 : width * tile_cols, :]
    rt_h[...], rt_l[...] = split(right)
    r_h[...], r_l[...] = split(right.T)
    lo[pl.ds(pl.multiple_of(col * lw, lw), lw), :] = l_ref[...]
    each(ncol, col, lambda p: left_gather(p, p).wait())

    @pl.loop(0, tile_rows // STEP)
    def _(g):
        lanes = pl.ds(pl.multiple_of(g * step_lanes, step_lanes), step_lanes)
        lp[lanes, :] = dot3(r_h[...], r_l[...], h_h[:, lanes], h_l[:, lanes]).T

    each(ncol, col, lambda p: left_term(p, col).start())
    lbuf[col] = lp[pl.ds(pl.multiple_of(col * lw, lw), lw), :]
    left = lo[...]
    lt_h[...], lt_l[...] = split(left)
    l_h[...], l_l[...] = split(left.T)

    blocks = width // STEP
    block_rows, block_cols = STEP * tile_cols, STEP * width
    chunks = block_cols // chunk

    @pl.loop(0, blocks)
    def _(k):
        b = lax.rem(row // chunks + 1 + k, blocks)
        rows = pl.ds(pl.multiple_of(b * block_rows, block_rows), block_rows)
        cols = pl.ds(pl.multiple_of(b * block_cols, block_cols), block_cols)
        o_scr[...] = dot3(rt_h[rows, :], rt_l[rows, :], l_h[...], l_l[...]) * scale
        for q in range(STEP // per):
            for i in range(tile_rows // per):
                pieces = [
                    o_scr[(q * per + a) * tile_cols : (q * per + a + 1) * tile_cols,
                          i * 128 : (i + 1) * 128]
                    for a in range(per)
                ]
                for a, piece in enumerate(swap_groups(pieces)):
                    at = (i * per + a) * tile_cols
                    high, low = split(piece)
                    t_h[at : at + tile_cols, q * 128 : (q + 1) * 128] = high
                    t_l[at : at + tile_cols, q * 128 : (q + 1) * 128] = low
        terms = dot3(ct_h[...], ct_l[...], t_h[...], t_l[...]).T
        for m in range(chunks):
            peer = b * chunks + m
            wp[peer, 0:chunk, :] = terms[m * chunk : (m + 1) * chunk, :]
            wp[peer, chunk : chunk + 8, :] = bias_tail

            @pl.when(peer != row)
            def _():
                weight_row_term(peer, row).start()

        pair_ref[...] += dot3(t_h[...], t_l[...], w_h[cols, :], w_l[cols, :])

    for d in range(width):
        rows = slice(d * tile_cols, (d + 1) * tile_cols)
        rp[pl.ds(d, tile_cols, stride=width), :] = dot3(
            h_h[rows, :], h_l[rows, :], lt_h[...], lt_l[...]
        )
    each(nrow, row, lambda p: weight_row_term(p, p).wait())
    wbuf[row] = wp[row]
    total = functools.reduce(lambda a, b: a + b, [wbuf[q] for q in range(nrow)])
    for q in range(ncol):
        part[0, q, 0:share, :] = total[q * share : (q + 1) * share, :]
        part[0, q, share : share + 8, :] = total[chunk : chunk + 8, :]
    each(ncol, col, lambda p: weight_col_term(p, col).start())
    each(nrow, row, lambda p: right_term(p, row).start())
    rbuf[row] = rp[pl.ds(pl.multiple_of(row * rw, rw), rw), :]
    part[1, col] = part[0, col]
    each(ncol, col, lambda p: weight_col_term(p, p).wait())
    total = functools.reduce(lambda a, b: a + b, [part[1, q] for q in range(ncol)])
    total = total / (tile_rows * nrow)
    wg_ref[row, col] = total[0:share, :]
    bg_ref[...] = total[share : share + 1, :]
    each(ncol, col, lambda p: weight_col_whole(p, col).start())
    each(ncol, col, lambda p: left_term(p, p).wait())
    lg_ref[...] = functools.reduce(lambda a, b: a + b, [lbuf[q] for q in range(ncol)])
    each(ncol, col, lambda p: weight_col_whole(p, p).wait())
    each(nrow, row, lambda p: weight_row_whole(p, row).start())
    each(nrow, row, lambda p: right_term(p, p).wait())
    rg_ref[...] = functools.reduce(lambda a, b: a + b, [rbuf[q] for q in range(nrow)])
    each(nrow, row, lambda p: weight_row_whole(p, p).wait())


def per_device(nrow, ncol, left_factors, right_factors, weight, bias, cotangent):
    samples, li, width = left_factors.shape
    rj = right_factors.shape[1]
    tile_rows, tile_cols, pair_width = cotangent.shape
    channels = weight.shape[0]
    lw, rw = li * width, rj * width
    lefts, rights = tile_rows * width, tile_cols * width
    chunk, share = channels // nrow, channels // (nrow * ncol)
    dma = pltpu.SemaphoreType.DMA

    def shape(*dims):
        return jax.ShapeDtypeStruct(dims, F32)

    def two(*dims):
        return [pltpu.VMEM(dims, BF16)] * 2

    def buf(*dims):
        return pltpu.VMEM(dims, F32)

    scratch = [
        buf(lefts, samples), buf(rights, samples),
        buf(lefts, samples), buf(ncol, lw, samples),
        buf(rights, samples), buf(nrow, rw, samples),
        buf(nrow, chunk + 8, pair_width), buf(nrow, chunk + 8, pair_width),
        buf(2, ncol, share + 8, pair_width),
        *two(samples, lefts), *two(lefts, samples),
        *two(samples, rights), *two(rights, samples),
        *two(channels, pair_width), *two(pair_width, channels),
        *two(tile_rows * tile_cols, pair_width), *two(pair_width, tile_rows * tile_cols),
        *two(rights, lefts),
        buf(STEP * tile_cols, lefts), *two(tile_rows * tile_cols, STEP * width),
        buf(max(rights, channels), 128),
    ]
    for count in (ncol, nrow, ncol, nrow, nrow, ncol, ncol, nrow):
        scratch += [dma((count,)), dma((count,))]
    pair, lg, rg, wg, bg = pl.pallas_call(
        functools.partial(tile_kernel, nrow, ncol, width),
        out_shape=(
            shape(tile_rows * tile_cols, pair_width), shape(lw, samples), shape(rw, samples),
            shape(nrow, ncol, share, pair_width), shape(1, pair_width),
        ),
        in_specs=[VMEM] * 5,
        out_specs=[VMEM] * 5,
        scratch_shapes=scratch,
        compiler_params=pltpu.CompilerParams(collective_id=0, has_side_effects=True),
        name="tile",
    )(
        left_factors.transpose(1, 2, 0).reshape(lw, samples),
        right_factors.transpose(1, 2, 0).reshape(rw, samples),
        weight,
        bias.reshape(1, pair_width),
        cotangent.reshape(tile_rows * tile_cols, pair_width),
    )
    return (
        pair.reshape(tile_rows, tile_cols, pair_width),
        lg.reshape(li, width, samples).transpose(2, 0, 1),
        rg.reshape(rj, width, samples).transpose(2, 0, 1),
        wg.reshape(width, width, pair_width).transpose(1, 0, 2).reshape(channels, pair_width),
        bg.reshape(pair_width),
    )


def solution(mesh):
    nrow, ncol = mesh.shape["row"], mesh.shape["col"]
    in_specs = (
        P(None, ("row", "col"), None),
        P(None, ("col", "row"), None),
        P(),
        P(),
        P("row", "col", None),
    )
    out_specs = (
        P("row", "col", None),
        P(None, ("row", "col"), None),
        P(None, ("col", "row"), None),
        P(),
        P(),
    )
    return jax.shard_map(
        functools.partial(per_device, nrow, ncol),
        mesh=mesh, in_specs=in_specs, out_specs=out_specs, check_vma=False,
    )
```

```python
import functools

import jax
import jax.numpy as jnp
from jax import lax
from jax.experimental import pallas as pl
from jax.experimental.pallas import tpu as pltpu
from jax.sharding import PartitionSpec as P

F32 = jnp.float32
BF16 = jnp.bfloat16
MESH = pl.DeviceIdType.MESH
VMEM = pl.BlockSpec(memory_space=pltpu.VMEM)
STEP = 8


def split(x):
    high = x.astype(BF16)
    return high, (x - high.astype(F32)).astype(BF16)


def dot(a, b):
    return lax.dot_general(a, b, (((1,), (0,)), ((), ())), preferred_element_type=F32)


def dot3(a_high, a_low, b_high, b_low):
    return dot(a_high, b_high) + (dot(a_high, b_low) + dot(a_low, b_high))


def dot_wide(a_high, a_low, b_both):
    half = b_both.shape[1] // 2
    wide = dot(a_high, b_both)
    return wide[:, 0:half] + (wide[:, half:] + dot(a_low, b_both[:, 0:half]))


def swap_groups(pieces):
    lane = lax.broadcasted_iota(jnp.int32, pieces[0].shape, 1)
    low = lane < 64
    even = (lane & 32) == 0

    def far(a, b):
        moved = pltpu.roll(jnp.where(low, b, a), 64, 1)
        return jnp.where(low, a, moved), jnp.where(low, moved, b)

    def near(a, b):
        return (
            jnp.where(even, a, pltpu.roll(b, 32, 1)),
            jnp.where(even, pltpu.roll(a, 96, 1), b),
        )

    p0, p2 = far(pieces[0], pieces[2])
    p1, p3 = far(pieces[1], pieces[3])
    p0, p1 = near(p0, p1)
    p2, p3 = near(p2, p3)
    return p0, p1, p2, p3


def tile_kernel(
    nrow, ncol, width, l_ref, r_ref, w_ref, b_ref, cot_ref,
    pair_ref, lg_ref, rg_ref, wg_ref, bg_ref,
    lo, ro, lp, lbuf, rp, rbuf, wp, wbuf, part,
    l_c, l_l, lt_c, r_h, r_l, rt_c, w_c, wt_h, wt_l,
    c_h, c_l, ct_h, ct_l, h_h, h_l, o_scr, t_h, t_l, tmp,
    gls, glr, grs, grr, ls, lr, rs, rr, ws, wr, vs, vr, us, ur, xs, xr, fs, fr,
):
    row, col = lax.axis_index("row"), lax.axis_index("col")
    lw, samples = l_ref.shape
    rw = r_ref.shape[0]
    tile_rows, tile_cols = ncol * lw // width, nrow * rw // width
    channels, pair_width = w_ref.shape
    scale = 1.0 / samples
    per = 128 // width
    chunk = channels // nrow
    share = channels // (nrow * ncol)

    def in_row(peer):
        return {"row": peer, "col": col}

    def in_col(peer):
        return {"row": row, "col": peer}

    def block(ref, index, size):
        return ref.at[pl.ds(pl.multiple_of(index * size, size), size)]

    def each(count, here, act):
        @pl.loop(1, count)
        def _(k):
            act(lax.rem(here + k, count))

    def send(src, dst, send_sem, recv_sem, device):
        return pltpu.make_async_remote_copy(
            src_ref=src, dst_ref=dst, send_sem=send_sem, recv_sem=recv_sem,
            device_id=device, device_id_type=MESH,
        )

    def left_gather(peer, slot):
        return send(l_ref, block(lo, slot, lw), gls.at[peer], glr.at[slot], in_col(peer))

    def right_gather(peer, slot):
        return send(r_ref, block(ro, slot, rw), grs.at[peer], grr.at[slot], in_row(peer))

    def left_term(peer, slot):
        return send(block(lp, peer, lw), lbuf.at[slot], ls.at[peer], lr.at[slot], in_col(peer))

    def right_term(peer, slot):
        return send(block(rp, peer, rw), rbuf.at[slot], rs.at[peer], rr.at[slot], in_row(peer))

    def weight_row_term(peer, slot):
        return send(wp.at[peer], wbuf.at[slot], ws.at[peer], wr.at[slot], in_row(peer))

    def weight_col_term(peer, slot):
        return send(part.at[0, peer], part.at[1, slot], vs.at[peer], vr.at[slot], in_col(peer))

    def weight_col_whole(peer, slot):
        return send(wg_ref.at[row, col], wg_ref.at[row, slot], us.at[peer], ur.at[slot], in_col(peer))

    def weight_row_whole(peer, slot):
        return send(wg_ref.at[row], wg_ref.at[slot], xs.at[peer], xr.at[slot], in_row(peer))

    partner = row + 1 - 2 * lax.rem(row, 2)

    def weight_pass(index):
        return send(wg_ref.at[index], wg_ref.at[index], fs.at[index], fr.at[index], in_row(partner))

    def same_core(act):
        @pl.loop(1, nrow // 2)
        def _(k):
            act(lax.rem(row + 2 * k, nrow))

    barrier = pltpu.get_barrier_semaphore()
    each(ncol, col, lambda p: pl.semaphore_signal(
        barrier, inc=1, device_id=in_col(p), device_id_type=MESH))
    each(nrow, row, lambda p: pl.semaphore_signal(
        barrier, inc=1, device_id=in_row(p), device_id_type=MESH))
    pl.semaphore_wait(barrier, nrow + ncol - 2)
    each(ncol, col, lambda p: left_gather(p, col).start())
    each(nrow, row, lambda p: right_gather(p, row).start())

    for d in range(width):
        tmp[d * width : (d + 1) * width, :] = w_ref[pl.ds(d, width, stride=width), :]
    weight = tmp[0:channels, :]
    w_c[:, 0:pair_width], w_c[:, pair_width:] = split(weight)
    wt_h[...], wt_l[...] = split(weight.T)
    cot = cot_ref[...]
    c_h[...], c_l[...] = split(cot)
    ct_h[...], ct_l[...] = split(cot.T)
    bias_tail = jnp.broadcast_to(jnp.sum(cot, axis=0, keepdims=True), (8, pair_width))
    pair_ref[...] = jnp.broadcast_to(b_ref[...], pair_ref.shape)

    step_lanes, step_rows = STEP * width, STEP * tile_cols
    halves = step_lanes // 128

    @pl.loop(0, tile_rows // STEP)
    def _(g):
        rows = pl.ds(pl.multiple_of(g * step_rows, step_rows), step_rows)
        grad = dot3(c_h[rows, :], c_l[rows, :], wt_h[...], wt_l[...]) * scale
        for b in range(width // per):
            for half in range(halves):
                pieces = [
                    grad[(half * per + a) * tile_cols : (half * per + a + 1) * tile_cols,
                         b * 128 : (b + 1) * 128]
                    for a in range(per)
                ]
                lanes = pl.ds(pl.multiple_of(g * step_lanes + half * 128, 128), 128)
                for a, piece in enumerate(swap_groups(pieces)):
                    at = (b * per + a) * tile_cols
                    high, low = split(piece)
                    h_h[at : at + tile_cols, lanes] = high
                    h_l[at : at + tile_cols, lanes] = low

    ro[pl.ds(pl.multiple_of(row * rw, rw), rw), :] = r_ref[...]
    each(nrow, row, lambda p: right_gather(p, p).wait())
    for d in range(width):
        tmp[d * tile_cols : (d + 1) * tile_cols, :] = ro[pl.ds(d, tile_cols, stride=width), :]
    right = tmp[0 : width * tile_cols, :]
    rt_c[:, 0:samples], rt_c[:, samples:] = split(right)
    r_h[...], r_l[...] = split(right.T)
    lo[pl.ds(pl.multiple_of(col * lw, lw), lw), :] = l_ref[...]
    each(ncol, col, lambda p: left_gather(p, p).wait())

    @pl.loop(0, tile_rows // STEP)
    def _(g):
        lanes = pl.ds(pl.multiple_of(g * step_lanes, step_lanes), step_lanes)
        lp[lanes, :] = dot3(r_h[...], r_l[...], h_h[:, lanes], h_l[:, lanes]).T

    each(ncol, col, lambda p: left_term(p, col).start())
    lbuf[col] = lp[pl.ds(pl.multiple_of(col * lw, lw), lw), :]
    left = lo[...]
    lt_c[:, 0:samples], lt_c[:, samples:] = split(left)
    high, l_l[...] = split(left.T)
    l_c[0:samples, :] = high
    l_c[samples:, :] = high

    blocks = width // STEP
    block_rows, block_cols = STEP * tile_cols, STEP * width
    chunks = block_cols // chunk

    @pl.loop(0, blocks)
    def _(k):
        b = lax.rem(row // chunks + 1 + k, blocks)
        rows = pl.ds(pl.multiple_of(b * block_rows, block_rows), block_rows)
        cols = pl.ds(pl.multiple_of(b * block_cols, block_cols), block_cols)
        o_scr[...] = (
            dot(rt_c[rows, :], l_c[...]) + dot(rt_c[rows, 0:samples], l_l[...])
        ) * scale
        for q in range(STEP // per):
            for i in range(tile_rows // per):
                pieces = [
                    o_scr[(q * per + a) * tile_cols : (q * per + a + 1) * tile_cols,
                          i * 128 : (i + 1) * 128]
                    for a in range(per)
                ]
                for a, piece in enumerate(swap_groups(pieces)):
                    at = (i * per + a) * tile_cols
                    high, low = split(piece)
                    t_h[at : at + tile_cols, q * 128 : (q + 1) * 128] = high
                    t_l[at : at + tile_cols, q * 128 : (q + 1) * 128] = low
        terms = dot3(ct_h[...], ct_l[...], t_h[...], t_l[...]).T
        for m in range(chunks):
            peer = b * chunks + m
            wp[peer, 0:chunk, :] = terms[m * chunk : (m + 1) * chunk, :]
            wp[peer, chunk : chunk + 8, :] = bias_tail

            @pl.when(peer != row)
            def _():
                weight_row_term(peer, row).start()

        pair_ref[...] += dot_wide(t_h[...], t_l[...], w_c[cols, :])

    for d in range(width):
        rows = slice(d * tile_cols, (d + 1) * tile_cols)
        rp[pl.ds(d, tile_cols, stride=width), :] = dot_wide(h_h[rows, :], h_l[rows, :], lt_c[...])
    each(nrow, row, lambda p: weight_row_term(p, p).wait())
    wbuf[row] = wp[row]
    total = functools.reduce(lambda a, b: a + b, [wbuf[q] for q in range(nrow)])
    for q in range(ncol):
        part[0, q, 0:share, :] = total[q * share : (q + 1) * share, :]
        part[0, q, share : share + 8, :] = total[chunk : chunk + 8, :]
    each(ncol, col, lambda p: weight_col_term(p, col).start())
    each(nrow, row, lambda p: right_term(p, row).start())
    rbuf[row] = rp[pl.ds(pl.multiple_of(row * rw, rw), rw), :]
    part[1, col] = part[0, col]
    each(ncol, col, lambda p: weight_col_term(p, p).wait())
    total = functools.reduce(lambda a, b: a + b, [part[1, q] for q in range(ncol)])
    total = total / (tile_rows * nrow)
    wg_ref[row, col] = total[0:share, :]
    bg_ref[...] = total[share : share + 1, :]
    each(ncol, col, lambda p: weight_col_whole(p, col).start())
    each(ncol, col, lambda p: left_term(p, p).wait())
    lg_ref[...] = functools.reduce(lambda a, b: a + b, [lbuf[q] for q in range(ncol)])
    each(ncol, col, lambda p: weight_col_whole(p, p).wait())
    weight_pass(row).start()
    same_core(lambda p: weight_row_whole(p, row).start())

    def pass_on(p):
        weight_row_whole(p, p).wait_recv()
        weight_pass(p).start()

    same_core(pass_on)
    each(nrow, row, lambda p: right_term(p, p).wait())
    rg_ref[...] = functools.reduce(lambda a, b: a + b, [rbuf[q] for q in range(nrow)])
    same_core(lambda p: weight_row_whole(p, p).wait_send())

    @pl.loop(0, nrow // 2)
    def _(k):
        weight_pass(lax.rem(row + 2 * k, nrow)).wait_send()
        weight_pass(lax.rem(partner + 2 * k, nrow)).wait_recv()


def finish_kernel(
    width, pair_ref, lg_ref, rg_ref, wg_ref, bg_ref,
    pair_out, lg_out, rg_out, w_out, bg_out, held, sems,
):
    copies = [
        pltpu.make_async_copy(src, dst, sems.at[k])
        for k, (src, dst) in enumerate([
            (wg_ref, held), (pair_ref, pair_out), (lg_ref, lg_out), (rg_ref, rg_out), (bg_ref, bg_out),
        ])
    ]
    for copy in copies:
        copy.start()
    copies[0].wait()
    nrow, ncol, share, _ = held.shape
    for r in range(nrow):
        for q in range(ncol):
            d, c = divmod((r * ncol + q) * share, width)
            w_out[pl.ds(c * width + d, share, stride=width), :] = held[r, q]
    for copy in copies[1:]:
        copy.wait()


def per_device(nrow, ncol, left_factors, right_factors, weight, bias, cotangent):
    samples, li, width = left_factors.shape
    rj = right_factors.shape[1]
    tile_rows, tile_cols, pair_width = cotangent.shape
    channels = weight.shape[0]
    lw, rw = li * width, rj * width
    lefts, rights = tile_rows * width, tile_cols * width
    chunk, share = channels // nrow, channels // (nrow * ncol)
    dma = pltpu.SemaphoreType.DMA

    def shape(*dims):
        return jax.ShapeDtypeStruct(dims, F32)

    def two(*dims):
        return [pltpu.VMEM(dims, BF16)] * 2

    def buf(*dims):
        return pltpu.VMEM(dims, F32)

    scratch = [
        buf(lefts, samples), buf(rights, samples),
        buf(lefts, samples), buf(ncol, lw, samples),
        buf(rights, samples), buf(nrow, rw, samples),
        buf(nrow, chunk + 8, pair_width), buf(nrow, chunk + 8, pair_width),
        buf(2, ncol, share + 8, pair_width),
        pltpu.VMEM((2 * samples, lefts), BF16), pltpu.VMEM((samples, lefts), BF16),
        pltpu.VMEM((lefts, 2 * samples), BF16),
        *two(samples, rights), pltpu.VMEM((rights, 2 * samples), BF16),
        pltpu.VMEM((channels, 2 * pair_width), BF16), *two(pair_width, channels),
        *two(tile_rows * tile_cols, pair_width), *two(pair_width, tile_rows * tile_cols),
        *two(rights, lefts),
        buf(STEP * tile_cols, lefts), *two(tile_rows * tile_cols, STEP * width),
        buf(max(rights, channels), 128),
    ]
    for count in (ncol, nrow, ncol, nrow, nrow, ncol, ncol, nrow, nrow):
        scratch += [dma((count,)), dma((count,))]
    pair, lg, rg, wg, bg = pl.pallas_call(
        functools.partial(tile_kernel, nrow, ncol, width),
        out_shape=(
            shape(tile_rows * tile_cols, pair_width), shape(lw, samples), shape(rw, samples),
            shape(nrow, ncol, share, pair_width), shape(1, pair_width),
        ),
        in_specs=[VMEM] * 5,
        out_specs=[VMEM] * 5,
        scratch_shapes=scratch,
        compiler_params=pltpu.CompilerParams(collective_id=0, has_side_effects=True),
        name="tile",
    )(
        left_factors.transpose(1, 2, 0).reshape(lw, samples),
        right_factors.transpose(1, 2, 0).reshape(rw, samples),
        weight,
        bias.reshape(1, pair_width),
        cotangent.reshape(tile_rows * tile_cols, pair_width),
    )
    whole = pl.BlockSpec(memory_space=pl.ANY)
    pair, lg, rg, wg, bg = pl.pallas_call(
        functools.partial(finish_kernel, width),
        out_shape=(
            shape(tile_rows * tile_cols, pair_width), shape(lw, samples), shape(rw, samples),
            shape(channels, pair_width), shape(1, pair_width),
        ),
        in_specs=[whole] * 5,
        out_specs=[VMEM] * 5,
        scratch_shapes=[buf(nrow, ncol, share, pair_width), dma((5,))],
        name="finish",
    )(pair, lg, rg, wg, bg)
    return (
        pair.reshape(tile_rows, tile_cols, pair_width),
        lg.reshape(li, width, samples).transpose(2, 0, 1),
        rg.reshape(rj, width, samples).transpose(2, 0, 1),
        wg,
        bg.reshape(pair_width),
    )


def solution(mesh):
    nrow, ncol = mesh.shape["row"], mesh.shape["col"]
    in_specs = (
        P(None, ("row", "col"), None),
        P(None, ("col", "row"), None),
        P(),
        P(),
        P("row", "col", None),
    )
    out_specs = (
        P("row", "col", None),
        P(None, ("row", "col"), None),
        P(None, ("col", "row"), None),
        P(),
        P(),
    )
    return jax.shard_map(
        functools.partial(per_device, nrow, ncol),
        mesh=mesh, in_specs=in_specs, out_specs=out_specs, check_vma=False,
    )
```

```python
import functools

import jax
import jax.numpy as jnp
from jax import lax
from jax.experimental import pallas as pl
from jax.experimental.pallas import tpu as pltpu
from jax.sharding import PartitionSpec as P

F32 = jnp.float32
BF16 = jnp.bfloat16
MESH = pl.DeviceIdType.MESH
VMEM = pl.BlockSpec(memory_space=pltpu.VMEM)
STEP = 8


def split(x):
    high = x.astype(BF16)
    return high, (x - high.astype(F32)).astype(BF16)


def dot(a, b):
    return lax.dot_general(a, b, (((1,), (0,)), ((), ())), preferred_element_type=F32)


def dot3(a_high, a_low, b_high, b_low):
    return dot(a_high, b_high) + (dot(a_high, b_low) + dot(a_low, b_high))


def dot_wide(a_high, a_low, b_both):
    half = b_both.shape[1] // 2
    wide = dot(a_high, b_both)
    return wide[:, 0:half] + (wide[:, half:] + dot(a_low, b_both[:, 0:half]))


def swap_groups(pieces):
    lane = lax.broadcasted_iota(jnp.int32, pieces[0].shape, 1)
    low = lane < 64
    even = (lane & 32) == 0

    def far(a, b):
        moved = pltpu.roll(jnp.where(low, b, a), 64, 1)
        return jnp.where(low, a, moved), jnp.where(low, moved, b)

    def near(a, b):
        return (
            jnp.where(even, a, pltpu.roll(b, 32, 1)),
            jnp.where(even, pltpu.roll(a, 96, 1), b),
        )

    p0, p2 = far(pieces[0], pieces[2])
    p1, p3 = far(pieces[1], pieces[3])
    p0, p1 = near(p0, p1)
    p2, p3 = near(p2, p3)
    return p0, p1, p2, p3


def tile_kernel(
    nrow, ncol, width, l_ref, r_ref, w_ref, b_ref, cot_ref,
    pair_ref, lg_ref, rg_ref, wg_ref, bg_ref,
    lo, ro, lp, lbuf, rp, rbuf, wp, wbuf, part,
    l_c, l_l, lt_c, r_h, r_l, rt_c, w_c, wt_h, wt_l,
    c_h, c_l, ct_h, ct_l, h_h, h_l, o_scr, t_h, t_l, tmp,
    gls, glr, grs, grr, ls, lr, rs, rr, ws, wr, vs, vr, us, ur, xs, xr, fs, fr,
):
    row, col = lax.axis_index("row"), lax.axis_index("col")
    lw, samples = l_ref.shape
    rw = r_ref.shape[0]
    tile_rows, tile_cols = ncol * lw // width, nrow * rw // width
    channels, pair_width = w_ref.shape
    scale = 1.0 / samples
    per = 128 // width
    chunk = channels // nrow
    share = channels // (nrow * ncol)

    def in_row(peer):
        return {"row": peer, "col": col}

    def in_col(peer):
        return {"row": row, "col": peer}

    def block(ref, index, size):
        return ref.at[pl.ds(pl.multiple_of(index * size, size), size)]

    def each(count, here, act):
        @pl.loop(1, count)
        def _(k):
            act(lax.rem(here + k, count))

    def send(src, dst, send_sem, recv_sem, device):
        return pltpu.make_async_remote_copy(
            src_ref=src, dst_ref=dst, send_sem=send_sem, recv_sem=recv_sem,
            device_id=device, device_id_type=MESH,
        )

    def left_gather(peer, slot):
        return send(l_ref, block(lo, slot, lw), gls.at[peer], glr.at[slot], in_col(peer))

    def right_gather(peer, slot):
        return send(r_ref, block(ro, slot, rw), grs.at[peer], grr.at[slot], in_row(peer))

    def left_term(peer, slot):
        return send(block(lp, peer, lw), lbuf.at[slot], ls.at[peer], lr.at[slot], in_col(peer))

    def right_term(peer, slot):
        return send(block(rp, peer, rw), rbuf.at[slot], rs.at[peer], rr.at[slot], in_row(peer))

    def weight_row_term(peer, slot):
        return send(wp.at[peer], wbuf.at[slot], ws.at[peer], wr.at[slot], in_row(peer))

    def weight_col_term(peer, slot):
        return send(part.at[0, peer], part.at[1, slot], vs.at[peer], vr.at[slot], in_col(peer))

    def weight_col_whole(peer, slot):
        return send(wg_ref.at[row, col], wg_ref.at[row, slot], us.at[peer], ur.at[slot], in_col(peer))

    def weight_row_whole(peer, slot):
        return send(wg_ref.at[row], wg_ref.at[slot], xs.at[peer], xr.at[slot], in_row(peer))

    partner = row + 1 - 2 * lax.rem(row, 2)

    def weight_pass(index):
        return send(wg_ref.at[index], wg_ref.at[index], fs.at[index], fr.at[index], in_row(partner))

    def same_core(act):
        @pl.loop(1, nrow // 2)
        def _(k):
            act(lax.rem(row + 2 * k, nrow))

    barrier = pltpu.get_barrier_semaphore()
    each(ncol, col, lambda p: pl.semaphore_signal(
        barrier, inc=1, device_id=in_col(p), device_id_type=MESH))
    each(nrow, row, lambda p: pl.semaphore_signal(
        barrier, inc=1, device_id=in_row(p), device_id_type=MESH))
    pl.semaphore_wait(barrier, nrow + ncol - 2)
    each(ncol, col, lambda p: left_gather(p, col).start())
    each(nrow, row, lambda p: right_gather(p, row).start())

    for d in range(width):
        tmp[d * width : (d + 1) * width, :] = w_ref[pl.ds(d, width, stride=width), :]
    weight = tmp[0:channels, :]
    w_c[:, 0:pair_width], w_c[:, pair_width:] = split(weight)
    wt_h[...], wt_l[...] = split(weight.T)
    cot = cot_ref[...]
    c_h[...], c_l[...] = split(cot)
    ct_h[...], ct_l[...] = split(cot.T)
    bias_tail = jnp.broadcast_to(jnp.sum(cot, axis=0, keepdims=True), (8, pair_width))
    pair_ref[...] = jnp.broadcast_to(b_ref[...], pair_ref.shape)

    step_lanes, step_rows = STEP * width, STEP * tile_cols
    halves = step_lanes // 128

    @pl.loop(0, tile_rows // STEP)
    def _(g):
        rows = pl.ds(pl.multiple_of(g * step_rows, step_rows), step_rows)
        grad = dot3(c_h[rows, :], c_l[rows, :], wt_h[...], wt_l[...]) * scale
        for b in range(width // per):
            for half in range(halves):
                pieces = [
                    grad[(half * per + a) * tile_cols : (half * per + a + 1) * tile_cols,
                         b * 128 : (b + 1) * 128]
                    for a in range(per)
                ]
                lanes = pl.ds(pl.multiple_of(g * step_lanes + half * 128, 128), 128)
                for a, piece in enumerate(swap_groups(pieces)):
                    at = (b * per + a) * tile_cols
                    high, low = split(piece)
                    h_h[at : at + tile_cols, lanes] = high
                    h_l[at : at + tile_cols, lanes] = low

    ro[pl.ds(pl.multiple_of(row * rw, rw), rw), :] = r_ref[...]
    each(nrow, row, lambda p: right_gather(p, p).wait())
    for d in range(width):
        tmp[d * tile_cols : (d + 1) * tile_cols, :] = ro[pl.ds(d, tile_cols, stride=width), :]
    right = tmp[0 : width * tile_cols, :]
    rt_c[:, 0:samples], rt_c[:, samples:] = split(right)
    r_h[...], r_l[...] = split(right.T)
    lo[pl.ds(pl.multiple_of(col * lw, lw), lw), :] = l_ref[...]
    each(ncol, col, lambda p: left_gather(p, p).wait())

    @pl.loop(0, tile_rows // STEP)
    def _(g):
        lanes = pl.ds(pl.multiple_of(g * step_lanes, step_lanes), step_lanes)
        lp[lanes, :] = dot3(r_h[...], r_l[...], h_h[:, lanes], h_l[:, lanes]).T

    each(ncol, col, lambda p: left_term(p, col).start())
    lbuf[col] = lp[pl.ds(pl.multiple_of(col * lw, lw), lw), :]
    left = lo[...]
    lt_c[:, 0:samples], lt_c[:, samples:] = split(left)
    high, l_l[...] = split(left.T)
    l_c[0:samples, :] = high
    l_c[samples:, :] = high

    blocks = width // STEP
    block_rows, block_cols = STEP * tile_cols, STEP * width
    chunks = block_cols // chunk

    @pl.loop(0, blocks)
    def _(k):
        b = lax.rem(row // chunks + 1 + k, blocks)
        rows = pl.ds(pl.multiple_of(b * block_rows, block_rows), block_rows)
        cols = pl.ds(pl.multiple_of(b * block_cols, block_cols), block_cols)
        o_scr[...] = (
            dot(rt_c[rows, :], l_c[...]) + dot(rt_c[rows, 0:samples], l_l[...])
        ) * scale
        for q in range(STEP // per):
            for i in range(tile_rows // per):
                pieces = [
                    o_scr[(q * per + a) * tile_cols : (q * per + a + 1) * tile_cols,
                          i * 128 : (i + 1) * 128]
                    for a in range(per)
                ]
                for a, piece in enumerate(swap_groups(pieces)):
                    at = (i * per + a) * tile_cols
                    high, low = split(piece)
                    t_h[at : at + tile_cols, q * 128 : (q + 1) * 128] = high
                    t_l[at : at + tile_cols, q * 128 : (q + 1) * 128] = low
        terms = dot3(ct_h[...], ct_l[...], t_h[...], t_l[...]).T
        for m in range(chunks):
            peer = b * chunks + m
            wp[peer, 0:chunk, :] = terms[m * chunk : (m + 1) * chunk, :]
            wp[peer, chunk : chunk + 8, :] = bias_tail

            @pl.when(peer != row)
            def _():
                weight_row_term(peer, row).start()

        pair_ref[...] += dot_wide(t_h[...], t_l[...], w_c[cols, :])

    for d in range(width):
        rows = slice(d * tile_cols, (d + 1) * tile_cols)
        rp[pl.ds(d, tile_cols, stride=width), :] = dot_wide(h_h[rows, :], h_l[rows, :], lt_c[...])
    each(nrow, row, lambda p: weight_row_term(p, p).wait())
    wbuf[row] = wp[row]
    total = functools.reduce(lambda a, b: a + b, [wbuf[q] for q in range(nrow)])
    for q in range(ncol):
        part[0, q, 0:share, :] = total[q * share : (q + 1) * share, :]
        part[0, q, share : share + 8, :] = total[chunk : chunk + 8, :]
    each(ncol, col, lambda p: weight_col_term(p, col).start())
    each(nrow, row, lambda p: right_term(p, row).start())
    rbuf[row] = rp[pl.ds(pl.multiple_of(row * rw, rw), rw), :]
    part[1, col] = part[0, col]
    each(ncol, col, lambda p: weight_col_term(p, p).wait())
    total = functools.reduce(lambda a, b: a + b, [part[1, q] for q in range(ncol)])
    total = total / (tile_rows * nrow)
    wg_ref[row, col] = total[0:share, :]
    bg_ref[...] = total[share : share + 1, :]
    each(ncol, col, lambda p: weight_col_whole(p, col).start())
    each(ncol, col, lambda p: weight_col_whole(p, p).wait())
    weight_pass(row).start()
    same_core(lambda p: weight_row_whole(p, row).start())

    each(ncol, col, lambda p: left_term(p, p).wait())
    lg_ref[...] = functools.reduce(lambda a, b: a + b, [lbuf[q] for q in range(ncol)])

    def pass_on(p):
        weight_row_whole(p, p).wait_recv()
        weight_pass(p).start()

    same_core(pass_on)
    each(nrow, row, lambda p: right_term(p, p).wait())
    rg_ref[...] = functools.reduce(lambda a, b: a + b, [rbuf[q] for q in range(nrow)])
    same_core(lambda p: weight_row_whole(p, p).wait_send())

    @pl.loop(0, nrow // 2)
    def _(k):
        weight_pass(lax.rem(row + 2 * k, nrow)).wait_send()
        weight_pass(lax.rem(partner + 2 * k, nrow)).wait_recv()


def finish_kernel(
    width, pair_ref, lg_ref, rg_ref, wg_ref, bg_ref,
    pair_out, lg_out, rg_out, w_out, bg_out, held, sems,
):
    copies = [
        pltpu.make_async_copy(src, dst, sems.at[k])
        for k, (src, dst) in enumerate([
            (wg_ref, held), (pair_ref, pair_out), (lg_ref, lg_out), (rg_ref, rg_out), (bg_ref, bg_out),
        ])
    ]
    for copy in copies:
        copy.start()
    copies[0].wait()
    nrow, ncol, share, _ = held.shape
    for r in range(nrow):
        for q in range(ncol):
            d, c = divmod((r * ncol + q) * share, width)
            w_out[pl.ds(c * width + d, share, stride=width), :] = held[r, q]
    for copy in copies[1:]:
        copy.wait()


def per_device(nrow, ncol, left_factors, right_factors, weight, bias, cotangent):
    samples, li, width = left_factors.shape
    rj = right_factors.shape[1]
    tile_rows, tile_cols, pair_width = cotangent.shape
    channels = weight.shape[0]
    lw, rw = li * width, rj * width
    lefts, rights = tile_rows * width, tile_cols * width
    chunk, share = channels // nrow, channels // (nrow * ncol)
    dma = pltpu.SemaphoreType.DMA

    def shape(*dims):
        return jax.ShapeDtypeStruct(dims, F32)

    def two(*dims):
        return [pltpu.VMEM(dims, BF16)] * 2

    def buf(*dims):
        return pltpu.VMEM(dims, F32)

    scratch = [
        buf(lefts, samples), buf(rights, samples),
        buf(lefts, samples), buf(ncol, lw, samples),
        buf(rights, samples), buf(nrow, rw, samples),
        buf(nrow, chunk + 8, pair_width), buf(nrow, chunk + 8, pair_width),
        buf(2, ncol, share + 8, pair_width),
        pltpu.VMEM((2 * samples, lefts), BF16), pltpu.VMEM((samples, lefts), BF16),
        pltpu.VMEM((lefts, 2 * samples), BF16),
        *two(samples, rights), pltpu.VMEM((rights, 2 * samples), BF16),
        pltpu.VMEM((channels, 2 * pair_width), BF16), *two(pair_width, channels),
        *two(tile_rows * tile_cols, pair_width), *two(pair_width, tile_rows * tile_cols),
        *two(rights, lefts),
        buf(STEP * tile_cols, lefts), *two(tile_rows * tile_cols, STEP * width),
        buf(max(rights, channels), 128),
    ]
    for count in (ncol, nrow, ncol, nrow, nrow, ncol, ncol, nrow, nrow):
        scratch += [dma((count,)), dma((count,))]
    pair, lg, rg, wg, bg = pl.pallas_call(
        functools.partial(tile_kernel, nrow, ncol, width),
        out_shape=(
            shape(tile_rows * tile_cols, pair_width), shape(lw, samples), shape(rw, samples),
            shape(nrow, ncol, share, pair_width), shape(1, pair_width),
        ),
        in_specs=[VMEM] * 5,
        out_specs=[VMEM] * 5,
        scratch_shapes=scratch,
        compiler_params=pltpu.CompilerParams(collective_id=0, has_side_effects=True),
        name="tile",
    )(
        left_factors.transpose(1, 2, 0).reshape(lw, samples),
        right_factors.transpose(1, 2, 0).reshape(rw, samples),
        weight,
        bias.reshape(1, pair_width),
        cotangent.reshape(tile_rows * tile_cols, pair_width),
    )
    whole = pl.BlockSpec(memory_space=pl.ANY)
    pair, lg, rg, wg, bg = pl.pallas_call(
        functools.partial(finish_kernel, width),
        out_shape=(
            shape(tile_rows * tile_cols, pair_width), shape(lw, samples), shape(rw, samples),
            shape(channels, pair_width), shape(1, pair_width),
        ),
        in_specs=[whole] * 5,
        out_specs=[VMEM] * 5,
        scratch_shapes=[buf(nrow, ncol, share, pair_width), dma((5,))],
        name="finish",
    )(pair, lg, rg, wg, bg)
    return (
        pair.reshape(tile_rows, tile_cols, pair_width),
        lg.reshape(li, width, samples).transpose(2, 0, 1),
        rg.reshape(rj, width, samples).transpose(2, 0, 1),
        wg,
        bg.reshape(pair_width),
    )


def solution(mesh):
    nrow, ncol = mesh.shape["row"], mesh.shape["col"]
    in_specs = (
        P(None, ("row", "col"), None),
        P(None, ("col", "row"), None),
        P(),
        P(),
        P("row", "col", None),
    )
    out_specs = (
        P("row", "col", None),
        P(None, ("row", "col"), None),
        P(None, ("col", "row"), None),
        P(),
        P(),
    )
    return jax.shard_map(
        functools.partial(per_device, nrow, ncol),
        mesh=mesh, in_specs=in_specs, out_specs=out_specs, check_vma=False,
    )
```
